32 devices in a mesh: gz: 8 (over z, y), gy: 4 (over x, core).
Axes of the slice: x: 2, y: 2, z: 4, core: 2. Of those that a mesh axis runs over, the one named last changes fastest.
Arguments:
- block: float32 [8, 64, 128, 256], P(None, 'gz', 'gy'), may hold values from -6 to 6
- conduct: float32 [64, 128, 256], P('gz', 'gy'), may hold values from 0.5 to 2
Outputs:
- basis: float32 [8, 64, 128, 256], P(None, 'gz', 'gy')
The draws below stay inside these ranges and needn't reach their ends.
All inputs are finite; a program needn't handle non-finite values.
Results may differ from the reference program's by a relative error of at most 0.00021.
Values sent between devices are 32-bit elements; how exact they have to be, the bound alone decides.
A program may use at most 128 MiB of HBM per device.

```python
import math
import jax
import jax.numpy as jnp
from jax import lax

VEC = 8
DEG = 4
NX = 256
NY = 128
NZ = 64


def steps_of(rng, shape, pieces, low, high):
    gain, own = 1.0, jax.random.fold_in(rng, 6)
    for position, shards_of in pieces:
        steps = jnp.exp(jax.random.uniform(jax.random.fold_in(own, position), (shards_of,), jnp.float32, low / len(pieces), high / len(pieces)))
        gain = gain * jnp.repeat(steps, shape[position] // shards_of).reshape([-1 if axis == position else 1 for axis in range(len(shape))])
    return gain


def gaussian(stream_key, extent, width, reach, split=(), held_as=jnp.bfloat16):
    result = jax.random.normal(stream_key, extent, jnp.float32) * width
    if len(split) > 0:
        result = steps_of(stream_key, extent, split, -0.22, 0.18) * result
    return jnp.clip(result, min=-reach, max=reach).astype(held_as)


def setup_inputs(seed: int = 0) -> dict:
    key_of = jax.random.split(jax.random.key(seed), 3)
    return {
        "block": gaussian(key_of[0], (VEC, NZ, NY, NX), 1.0, 6.0, ((1, 8), (2, 4)), jnp.float32),
        "conduct": jnp.clip(jnp.exp(math.log(2.0) - 1.3862944 * jax.random.uniform(key_of[1], (NZ, NY, NX), jnp.float32) ** steps_of(key_of[1], (NZ, NY, NX), ((0, 8), (1, 4)), -0.2, 0.2)), 0.5, 2.0),
    }


mid_point = 12.75
half_width = 11.25

def stencil(padded, kpadded):
    inner = slice(1, -1)
    centre = padded[:, 1:-1, 1:-1, 1:-1]
    kcentre = kpadded[1:-1, 1:-1, 1:-1]
    shifts = [(slice(2, None), inner, inner), (slice(None, -2), inner, inner), (inner, slice(2, None), inner), (inner, slice(None, -2), inner), (inner, inner, slice(2, None)), (inner, inner, slice(None, -2))]
    total = jnp.zeros_like(centre)
    for where in shifts:
        total = total + 0.5 * (kcentre + kpadded[where]) * (centre - padded[(slice(None),) + where])
    return total

def operate(field, conduct):
    padded = jnp.pad(field, ((0, 0), (1, 1), (1, 1), (1, 1)))
    kpadded = jnp.pad(conduct, 1)
    return stencil(padded, kpadded)

def reference(block, conduct):
    field = block
    for passes in range(2):
        previous = field
        current = (operate(field, conduct) - mid_point * field) / half_width
        for step in range(DEG - 1):
            nextone = 2.0 * (operate(current, conduct) - mid_point * current) / half_width - previous
            previous = current
            current = nextone
        field = current
    vectors = field.shape[0]
    flat = field.reshape(vectors, -1)
    gram = jnp.dot(flat, flat.T, precision=lax.Precision.HIGHEST)
    lower = jnp.linalg.cholesky(gram)
    inverse = lax.linalg.triangular_solve(lower, jnp.eye(vectors, dtype=jnp.float32), left_side=True, lower=True)
    scaled = jnp.dot(inverse, flat, precision=lax.Precision.HIGHEST) * math.sqrt(flat.shape[1])
    return scaled.reshape(field.shape)
```

```python
import functools
import math

import jax
import jax.numpy as jnp
from jax import lax
from jax.experimental import pallas as pl
from jax.experimental.pallas import tpu as pltpu
from jax.sharding import PartitionSpec as P

DEG = 4
PASSES = 2
STEPS = DEG * PASSES
CHUNKS = 2
TILE = 8

mid_point = 12.75
half_width = 11.25


def weigh(coef, weights, rows, low_y, high_y):
    wz, wym, wyp, wxm, wxp, diag = weights
    span, tall, columns = coef.shape
    scale = 1.0 / half_width
    row_id = lax.broadcasted_iota(jnp.int32, (tall, columns), 0)
    col_id = lax.broadcasted_iota(jnp.int32, (tall, columns), 1)
    first_row, last_row = TILE, TILE + rows - 1
    cut_p = ((row_id == last_row) & jnp.logical_not(high_y)) | ((row_id == first_row - 1) & jnp.logical_not(low_y))
    cut_m = ((row_id == last_row + 1) & jnp.logical_not(high_y)) | ((row_id == first_row) & jnp.logical_not(low_y))
    first, last = col_id == 0, col_id == columns - 1
    wz[0] = scale * (coef[0] + coef[1])

    @pl.loop(1, span - 1)
    def _(z):
        plane = coef[z]
        yp = scale * (plane + pltpu.roll(plane, tall - 1, 0))
        ym = scale * (plane + pltpu.roll(plane, 1, 0))
        xp = scale * (plane + pltpu.roll(plane, columns - 1, 1))
        wz[z] = scale * (plane + coef[z + 1])
        xm = scale * (plane + pltpu.roll(plane, 1, 1))
        xp = jnp.where(last, 0.0, xp)
        xm = jnp.where(first, 0.0, xm)
        wxp[z] = xp
        wxm[z] = xm
        ends = jnp.where(first | last, scale * plane, 0.0)
        diag[z] = (yp + ym) + (xp + xm) + (ends - 2.0 * mid_point / half_width)
        wyp[z] = jnp.where(cut_p, 0.0, yp)
        wym[z] = jnp.where(cut_m, 0.0, ym)


def advance(now, prev, dst, weights, step):
    wz, wym, wyp, wxm, wxp, diag = weights
    span, tall, columns = now.shape
    tiles, wide = tall // TILE, columns // 128
    group = max(n for n in (1, 2, 3) if tiles % n == 0)
    row_id = lax.broadcasted_iota(jnp.int32, (TILE, 128), 0)
    col_id = lax.broadcasted_iota(jnp.int32, (TILE, 128), 1)
    top, bottom, start, end = row_id == 0, row_id == TILE - 1, col_id == 0, col_id == 127

    @pl.loop(0, tiles // group)
    def _(b):
        def offset(r):
            return pl.multiple_of((b * group + r + tiles) % tiles * TILE, TILE)

        rows = [offset(r) for r in range(-1, group + 1)]

        def at(ref, z, r, c):
            return ref[z, pl.ds(rows[r + 1], TILE), c * 128 : (c + 1) * 128]

        parts = [(r, c) for r in range(group) for c in range(wide)]
        current = {t: at(now, step, *t) for t in parts}
        flux = {t: at(wz, step - 1, *t) * (current[t] - at(now, step - 1, *t)) for t in parts}
        for z in range(step, span - step):
            further = {t: at(now, z + 1, *t) for t in parts}
            for r in range(group):
                lefts = [pltpu.roll(current[r, c], 1, 1) for c in range(wide)]
                rights = [pltpu.roll(current[r, c], 127, 1) for c in range(wide)]
                for c in range(wide):
                    mid = current[r, c]
                    below = current[r - 1, c] if r else at(now, z, -1, c)
                    above = current[r + 1, c] if r < group - 1 else at(now, z, group, c)
                    below = pltpu.roll(jnp.where(bottom, below, mid), 1, 0)
                    above = pltpu.roll(jnp.where(top, above, mid), TILE - 1, 0)
                    left = jnp.where(start, lefts[(c - 1) % wide], lefts[c])
                    right = jnp.where(end, rights[(c + 1) % wide], rights[c])
                    onward = at(wz, z, r, c) * (further[r, c] - mid)
                    total = at(diag, z, r, c) * mid + (flux[r, c] - onward)
                    total = total - (at(wym, z, r, c) * below + at(wyp, z, r, c) * above)
                    total = total - (at(wxm, z, r, c) * left + at(wxp, z, r, c) * right)
                    if prev is None:
                        total = 0.5 * total
                    else:
                        total = total - at(prev, z, r, c)
                    dst[z, pl.ds(rows[r + 1], TILE), c * 128 : (c + 1) * 128] = total
                    flux[r, c] = onward
            current = further


def steps_of(field, even, odd):
    held = [field]
    plan = []
    for step in range(1, STEPS + 1):
        dst = field if step == STEPS else (odd if step % 2 else even)
        first = step % DEG == 1
        plan.append((held[-1], None if first else held[-2], dst))
        held.append(dst)
    return plan


def kernel(
    nz, ny,
    block, conduct, filtered, gram_out,
    field, even, odd, coef, wz, wym, wyp, wxm, wxp, diag,
    gathered, pairs, gsum_y, gsum_z,
    outbox,
    lo, ll, xs, xr, es, er, fs, fr, ys, yr, rs, rr, rl, gys, gyr, gzs, gzr, outs,
):
    g = lax.axis_index("gz")
    h = lax.axis_index("gy")
    part = lax.rem(g, 2)
    other = 1 - part
    partner = g + 1 - 2 * part
    vectors, planes, rows, columns = block.shape
    mine = vectors // 2
    span, tall = 4 * planes, rows + 2 * TILE
    low_z, high_z = g >= 2, g < nz - 2
    low_y, high_y = h >= 1, h < ny - 1
    part_low = part == 0
    early_to, forward_to = g - 2 + 4 * part, g + 2 - 4 * part
    can_early = jnp.logical_or(jnp.logical_and(part_low, low_z), jnp.logical_and(jnp.logical_not(part_low), high_z))
    can_forward = jnp.logical_or(jnp.logical_and(part_low, high_z), jnp.logical_and(jnp.logical_not(part_low), low_z))
    begin = {
        "here": planes * (1 + part), "there": planes * (2 - part),
        "early": 3 * planes * other, "forward": 3 * planes * part,
    }
    regions = ("here", "there", "early", "forward")
    inner = pl.ds(TILE, rows)

    def remote(src, dst, send, recv, gz, gy):
        return pltpu.make_async_remote_copy(
            src_ref=src, dst_ref=dst, send_sem=send, recv_sem=recv,
            device_id={"gz": gz, "gy": gy}, device_id_type=pl.DeviceIdType.MESH,
        )

    barrier = pltpu.get_barrier_semaphore()
    for d in range(1, nz):
        pl.semaphore_signal(barrier, inc=1, device_id={"gz": lax.rem(g + d, nz), "gy": h}, device_id_type=pl.DeviceIdType.MESH)
    for d in range(1, ny):
        pl.semaphore_signal(barrier, inc=1, device_id={"gz": g, "gy": lax.rem(h + d, ny)}, device_id_type=pl.DeviceIdType.MESH)

    order = [mine] + list(range(mine))

    def body(i):
        return coef if isinstance(i, int) and i == mine else field.at[i]

    def source(i, side):
        return conduct if i == mine else block.at[mine * side + i]

    def local(i):
        return pltpu.make_async_copy(source(i, part), body(i).at[pl.ds(begin["here"], planes), inner], ll.at[i])

    def load(i):
        return pltpu.make_async_copy(source(i, other), outbox.at[i], lo.at[i])

    size = planes // CHUNKS

    def swap(i, k):
        return remote(
            outbox.at[i, pl.ds(k * size, size)], body(i).at[pl.ds(begin["here"] + k * size, size), inner],
            xs.at[i, k], xr.at[i, k], partner, h,
        )

    def swap_in(i, k):
        return remote(
            outbox.at[i, pl.ds(k * size, size)], body(i).at[pl.ds(begin["there"] + k * size, size), inner],
            xs.at[i, k], xr.at[i, k], partner, h,
        )

    def early(i):
        return remote(
            body(i).at[pl.ds(begin["here"], planes), inner], body(i).at[pl.ds(begin["early"], planes), inner],
            es.at[i], er.at[i], early_to, h,
        )

    def forward(i, k):
        return remote(
            body(i).at[pl.ds(begin["there"] + k * size, size), inner],
            body(i).at[pl.ds(begin["forward"] + k * size, size), inner],
            fs.at[i, k], fr.at[i, k], forward_to, h,
        )

    def row_copies(i, q, arriving):
        zs = pl.ds(begin[regions[q]], planes)
        data = body(i)
        down, up = (h + 1, h - 1) if arriving else (h - 1, h + 1)
        ok_down, ok_up = (high_y, low_y) if arriving else (low_y, high_y)
        return [
            (ok_down, remote(data.at[zs, pl.ds(TILE, TILE)], data.at[zs, pl.ds(TILE + rows, TILE)], ys.at[i, q, 0], yr.at[i, q, 0], g, down)),
            (ok_up, remote(data.at[zs, pl.ds(rows, TILE)], data.at[zs, pl.ds(0, TILE)], ys.at[i, q, 1], yr.at[i, q, 1], g, up)),
        ]

    exists = {0: None, 1: None, 2: can_forward, 3: can_early}

    def rows_do(i, q, what, arriving=False):
        for ok, copy in row_copies(i, q, arriving):
            if exists[q] is not None:
                ok = jnp.logical_and(ok, exists[q])
            pl.when(ok)(getattr(copy, what))

    for i in order:
        load(i).start()
    for i in order:
        local(i).start()

    blank = jnp.zeros((tall, columns), jnp.float32)
    edge = jnp.zeros((TILE, columns), jnp.float32)
    for name, exist in (("early", can_forward), ("forward", can_early)):
        @pl.when(jnp.logical_not(exist))
        def _():
            for i in order:
                @pl.loop(0, planes)
                def _(z):
                    body(i)[begin[name] + z] = blank
    for at, exist in ((0, low_y), (TILE + rows, high_y)):
        @pl.when(jnp.logical_not(exist))
        def _():
            for i in order:
                @pl.loop(0, span)
                def _(z):
                    body(i)[z, at : at + TILE, :] = edge

    pl.semaphore_wait(barrier, nz + ny - 2)
    for i in order:
        load(i).wait()
        for k in range(CHUNKS):
            swap(i, k).start()
    for i in order:
        local(i).wait()
        pl.when(can_early)(early(i).start)
        rows_do(i, 0, "start")

    def take(i, k):
        swap_in(i, k).wait_recv()
        pl.when(can_forward)(forward(i, k).start)
        if k == CHUNKS - 1:
            rows_do(i, 1, "start")

    def take_early(i):
        pl.when(can_forward)(early(i).wait_recv)
        rows_do(i, 2, "start")

    def take_forward(i):
        for k in range(CHUNKS):
            pl.when(can_early)(forward(i, k).wait_recv)
        rows_do(i, 3, "start")

    def ready(i):
        for q in range(4):
            rows_do(i, q, "wait_recv", True)

    def sent(i):
        for k in range(CHUNKS):
            pl.when(can_forward)(forward(i, k).wait_send)
        pl.when(can_early)(early(i).wait_send)
        for q in range(4):
            rows_do(i, q, "wait_send")

    take(mine, 0)
    take_early(mine)
    for k in range(1, CHUNKS):
        take(mine, k)
    take_early(0)
    take(0, 0)
    take_forward(mine)
    for k in range(1, CHUNKS):
        take(0, k)
    ready(mine)
    weights = (wz, wym, wyp, wxm, wxp, diag)
    weigh(coef, weights, rows, low_y, high_y)

    @pl.when(jnp.logical_not(low_z))
    def _():
        wz[planes - 1] = blank
        diag[planes] = diag[planes] + coef[planes] * (1.0 / half_width)

    @pl.when(jnp.logical_not(high_z))
    def _():
        wz[3 * planes - 1] = blank
        diag[3 * planes - 1] = diag[3 * planes - 1] + coef[3 * planes - 1] * (1.0 / half_width)

    events = {}

    def plan(v, step, *acts):
        events.setdefault((v, step), []).extend(acts)

    if mine > 1:
        plan(0, 0, lambda: take_early(1), lambda: take(1, 0))
    plan(0, 0, lambda: take_forward(0))
    if mine > 1:
        plan(0, 0, *[functools.partial(take, 1, k) for k in range(1, CHUNKS)])
    for v in range(1, mine):
        if v + 1 < mine:
            plan(v - 1, 2, functools.partial(take_early, v + 1), functools.partial(take, v + 1, 0))
        plan(v - 1, 5, functools.partial(take_forward, v))
        if v + 1 < mine:
            plan(v - 1, 5, *[functools.partial(take, v + 1, k) for k in range(1, CHUNKS)])

    def give_back(v):
        return remote(
            field.at[v, pl.ds(begin["there"], planes), inner], gathered.at[mine * part + v],
            rs.at[v], rr.at[v], partner, h,
        )

    def returned(v):
        return remote(
            field.at[v, pl.ds(begin["there"], planes), inner], gathered.at[mine * other + v],
            rs.at[v], rr.at[v], partner, h,
        )

    def keep(v):
        return pltpu.make_async_copy(
            field.at[v, pl.ds(begin["here"], planes), inner], gathered.at[mine * part + v], rl.at[v]
        )

    @pl.loop(0, mine)
    def _(v):
        plan = steps_of(field.at[v], even, odd)
        for step in range(STEPS + 1):
            if step:
                advance(*plan[step - 1], weights, step)
            for w in range(mine):
                if (w, step) in events:
                    @pl.when(v == w)
                    def _():
                        for act in events[w, step]:
                            act()
            if step == 0:
                ready(v)
            if step == STEPS - 1:
                sent(v)
        give_back(v).start()
        keep(v).start()

    for v in range(mine):
        keep(v).wait()
        returned(v).wait_recv()
    to_out = pltpu.make_async_copy(gathered, filtered, outs)
    to_out.start()

    index = [(i, j) for i in range(vectors) for j in range(i + 1)]
    tiles = rows // 8

    def gram_body(t, accs):
        z, r = t // tiles, pl.multiple_of((t % tiles) * 8, 8)
        accs = list(accs)
        for c in range(columns // 128):
            vals = [gathered[v, z, pl.ds(r, 8), c * 128 : (c + 1) * 128] for v in range(vectors)]
            for p, (i, j) in enumerate(index):
                accs[p] = accs[p] + vals[i] * vals[j]
        return tuple(accs)

    accs = lax.fori_loop(0, planes * tiles, gram_body, tuple(jnp.zeros((8, 128), jnp.float32) for _ in index))
    pairs[...] = jnp.zeros((128, 128), jnp.float32)
    for p, (i, j) in enumerate(index):
        line = jnp.sum(accs[p], axis=0, keepdims=True)
        pairs[i * vectors + j : i * vectors + j + 1, :] = line
        if i != j:
            pairs[j * vectors + i : j * vectors + i + 1, :] = line
    ones = jnp.ones((8, 128), jnp.float32)
    part_sum = lax.dot_general(
        ones, pairs[...], (((1,), (1,)), ((), ())), precision=lax.Precision.HIGHEST,
        preferred_element_type=jnp.float32,
    )

    def total_of(value, slots, send, recv, axis, me, count):
        slots[me] = value
        copies = []
        for d in range(1, count):
            target = lax.rem(me + d, count)
            gz, gy = (target, h) if axis == "gz" else (g, target)
            copy = remote(slots.at[me], slots.at[me], send.at[d - 1], recv.at[d - 1], gz, gy)
            copy.start()
            copies.append(copy)
        for d in range(1, count):
            source = lax.rem(me - d + count, count)
            gz, gy = (source, h) if axis == "gz" else (g, source)
            remote(slots.at[source], slots.at[source], send.at[d - 1], recv.at[d - 1], gz, gy).wait_recv()
        result = slots[0]
        for d in range(1, count):
            result = result + slots[d]
        for copy in copies:
            copy.wait_send()
        return result

    slab = total_of(part_sum, gsum_y, gys, gyr, "gy", h, ny)
    gram_out[...] = total_of(slab, gsum_z, gzs, gzr, "gz", g, nz)

    sent(mine)
    for i in order:
        for k in range(CHUNKS):
            swap(i, k).wait_send()
    for v in range(mine):
        give_back(v).wait_send()
    to_out.wait()


def filter_and_gram(block, conduct):
    nz, ny = lax.axis_size("gz"), lax.axis_size("gy")
    vectors, planes, rows, columns = block.shape
    mine, span, tall = vectors // 2, 4 * planes, rows + 2 * TILE
    f32 = jnp.float32
    dma = pltpu.SemaphoreType.DMA
    volume = pltpu.VMEM((span, tall, columns), f32)
    return pl.pallas_call(
        functools.partial(kernel, nz, ny),
        out_shape=[jax.ShapeDtypeStruct(block.shape, f32), jax.ShapeDtypeStruct((8, 128), f32)],
        in_specs=[pl.BlockSpec(memory_space=pl.ANY)] * 2,
        out_specs=[pl.BlockSpec(memory_space=pl.ANY), pl.BlockSpec(memory_space=pltpu.VMEM)],
        scratch_shapes=[
            pltpu.VMEM((mine, span, tall, columns), f32),
            volume, volume, volume, volume, volume, volume, volume, volume, volume,
            pltpu.VMEM((vectors, planes, rows, columns), f32),
            pltpu.VMEM((128, 128), f32),
            pltpu.VMEM((ny, 8, 128), f32),
            pltpu.VMEM((nz, 8, 128), f32),
            pltpu.VMEM((mine + 1, planes, rows, columns), f32),
            dma((mine + 1,)), dma((mine + 1,)),
            dma((mine + 1, CHUNKS)), dma((mine + 1, CHUNKS)),
            dma((mine + 1,)), dma((mine + 1,)),
            dma((mine + 1, CHUNKS)), dma((mine + 1, CHUNKS)),
            dma((mine + 1, 4, 2)), dma((mine + 1, 4, 2)),
            dma((mine,)), dma((mine,)), dma((mine,)),
            dma((ny,)), dma((ny,)), dma((nz,)), dma((nz,)),
            dma,
        ],
        compiler_params=pltpu.CompilerParams(
            collective_id=0, has_side_effects=True, vmem_limit_bytes=60 * 1024 * 1024
        ),
        name="filter_and_gram",
    )(block, conduct)


def finish_kernel(cells, sums, field, basis, held, result, taken, given):
    vectors, planes, rows, columns = field.shape
    take = [pltpu.make_async_copy(field.at[:, z], held.at[:, z], taken.at[z]) for z in range(planes)]
    give = [pltpu.make_async_copy(result.at[:, z], basis.at[:, z], given.at[z]) for z in range(planes)]
    for z in range(planes):
        take[z].start()
    gram = sums[...]
    low = {}
    factors = {}
    recip = []
    for j in range(vectors):
        for i in range(j, vectors):
            at = i * vectors + j
            value = jnp.broadcast_to(gram[:, at : at + 1], (8, 128))
            for k in range(j):
                value = value - low[i, k] * low[j, k]
            if i == j:
                low[j, j] = jnp.sqrt(value)
                recip.append(1.0 / low[j, j])
            else:
                low[i, j] = value * recip[j]
    for j in range(vectors):
        column = {j: recip[j]}
        for i in range(j + 1, vectors):
            value = low[i, j] * column[j]
            for k in range(j + 1, i):
                value = value + low[i, k] * column[k]
            column[i] = -value * recip[i]
        for i in range(j, vectors):
            factors[i, j] = column[i] * math.sqrt(cells)

    for z in range(planes):
        take[z].wait()

        @pl.loop(0, rows, step=8)
        def _(r):
            r = pl.multiple_of(r, 8)
            for c in range(0, columns, 128):
                vals = [held[v, z, pl.ds(r, 8), c : c + 128] for v in range(vectors)]
                for i in range(vectors):
                    total = factors[i, 0] * vals[0]
                    for j in range(1, i + 1):
                        total = total + factors[i, j] * vals[j]
                    result[i, z, pl.ds(r, 8), c : c + 128] = total

        give[z].start()
    for z in range(planes):
        give[z].wait()


def shards(block, conduct):
    vectors, planes, rows, columns = block.shape
    field, sums = filter_and_gram(block, conduct)
    total_cells = columns * rows * planes * lax.axis_size("gz") * lax.axis_size("gy")
    whole = pltpu.VMEM(block.shape, jnp.float32)
    return pl.pallas_call(
        functools.partial(finish_kernel, total_cells),
        out_shape=jax.ShapeDtypeStruct(block.shape, jnp.float32),
        in_specs=[pl.BlockSpec(memory_space=pltpu.VMEM), pl.BlockSpec(memory_space=pl.ANY)],
        out_specs=pl.BlockSpec(memory_space=pl.ANY),
        scratch_shapes=[whole, whole, pltpu.SemaphoreType.DMA((planes,)), pltpu.SemaphoreType.DMA((planes,))],
        compiler_params=pltpu.CompilerParams(vmem_limit_bytes=60 * 1024 * 1024),
        name="finish",
    )(sums, field)


def solution(mesh):
    in_specs = (P(None, "gz", "gy", None), P("gz", "gy", None))
    out_specs = P(None, "gz", "gy", None)
    return jax.shard_map(shards, mesh=mesh, in_specs=in_specs, out_specs=out_specs, check_vma=False)
```

```python
import functools
import math

import jax
import jax.numpy as jnp
from jax import lax
from jax.experimental import pallas as pl
from jax.experimental.pallas import tpu as pltpu
from jax.sharding import PartitionSpec as P

DEG = 4
PASSES = 2
STEPS = DEG * PASSES
CHUNKS = 2
TILE = 8

mid_point = 12.75
half_width = 11.25


def weigh(coef, weights, rows, low_y, high_y):
    wz, wy, wx, diag = weights
    span, tall, columns = coef.shape
    scale = 1.0 / half_width
    row_id = lax.broadcasted_iota(jnp.int32, (tall, columns), 0)
    col_id = lax.broadcasted_iota(jnp.int32, (tall, columns), 1)
    cut = ((row_id == TILE + rows - 1) & jnp.logical_not(high_y)) | ((row_id == TILE - 1) & jnp.logical_not(low_y))
    first, last = col_id == 0, col_id == columns - 1
    wz[0] = scale * (coef[0] + coef[1])

    @pl.loop(1, span - 1, unroll=2)
    def _(z):
        plane = scale * coef[z]
        yp = plane + pltpu.roll(plane, tall - 1, 0)
        ym = plane + pltpu.roll(plane, 1, 0)
        xp = plane + jnp.where(last, 0.0, pltpu.roll(plane, columns - 1, 1))
        xm = plane + jnp.where(first, 0.0, pltpu.roll(plane, 1, 1))
        wz[z] = plane + scale * coef[z + 1]
        wx[z] = jnp.where(last, 0.0, xp)
        wy[z] = jnp.where(cut, 0.0, yp)
        diag[z] = (yp + ym) + (xp + xm) - 2.0 * mid_point / half_width


def advance(now, prev, dst, weights, step):
    wz, wy, wx, diag = weights
    span, tall, columns = now.shape
    own, wide = tall // TILE - 2, columns // 128
    row_id = lax.broadcasted_iota(jnp.int32, (TILE, 128), 0)
    col_id = lax.broadcasted_iota(jnp.int32, (TILE, 128), 1)
    top, bottom, start, end = row_id == 0, row_id == TILE - 1, col_id == 0, col_id == 127

    def at(ref, z, r, c):
        return ref[z, r * TILE : (r + 1) * TILE, c * 128 : (c + 1) * 128]

    def sweep(tiles, low, high):
        parts = [(r, c) for r, _, _ in tiles for c in range(wide)]
        current = {t: at(now, low, *t) for t in parts}
        flux = {t: at(wz, low - 1, *t) * (current[t] - at(now, low - 1, *t)) for t in parts}
        for z in range(low, high):
            further = {t: at(now, z + 1, *t) for t in parts}
            weight = {t: at(wy, z, *t) for t in parts}
            product = {t: weight[t] * current[t] for t in parts}
            for r, smaller, larger in tiles:
                across = [at(wx, z, r, c) for c in range(wide)]
                lefts = [pltpu.roll(across[c] * current[r, c], 1, 1) for c in range(wide)]
                rights = [pltpu.roll(current[r, c], 127, 1) for c in range(wide)]
                for c in range(wide):
                    t = (r, c)
                    mid = current[t]
                    below = product[t] if smaller is None else product.get((smaller, c))
                    if below is None:
                        below = at(wy, z, smaller, c) * at(now, z, smaller, c)
                    above = mid if larger is None else current.get((larger, c))
                    if above is None:
                        above = at(now, z, larger, c)
                    below = pltpu.roll(jnp.where(bottom, below, product[t]), 1, 0)
                    above = pltpu.roll(jnp.where(top, above, mid), TILE - 1, 0)
                    left = jnp.where(start, lefts[(c - 1) % wide], lefts[c])
                    right = jnp.where(end, rights[(c + 1) % wide], rights[c])
                    onward = at(wz, z, *t) * (further[t] - mid)
                    total = at(diag, z, *t) * mid + (flux[t] - onward)
                    total = total - (below + weight[t] * above)
                    total = total - (left + across[c] * right)
                    if prev is None:
                        total = 0.5 * total
                    else:
                        total = total - at(prev, z, *t)
                    dst[z, r * TILE : (r + 1) * TILE, c * 128 : (c + 1) * 128] = total
                    flux[t] = onward
            current = further

    for r in range(1, own + 1, 4):
        sweep([(q, q - 1, q + 1) for q in range(r, min(r + 4, own + 1))], step, span - step)
    if step < STEPS:
        sweep([(0, None, 1), (own + 1, own, None)], step + 1, span - step - 1)


def steps_of(field, even, odd):
    held = [field]
    plan = []
    for step in range(1, STEPS + 1):
        dst = field if step == STEPS else (odd if step % 2 else even)
        first = step % DEG == 1
        plan.append((held[-1], None if first else held[-2], dst))
        held.append(dst)
    return plan


def kernel(
    nz, ny,
    block, conduct, filtered, gram_out,
    field, even, odd, coef, wz, wy, wx, diag,
    gathered, pairs, gsum_y, gsum_z,
    outbox,
    lo, ll, xs, xr, es, er, fs, fr, ys, yr, rs, rr, rl, gys, gyr, gzs, gzr, outs,
):
    g = lax.axis_index("gz")
    h = lax.axis_index("gy")
    part = lax.rem(g, 2)
    other = 1 - part
    partner = g + 1 - 2 * part
    vectors, planes, rows, columns = block.shape
    mine = vectors // 2
    span, tall = 4 * planes, rows + 2 * TILE
    low_z, high_z = g >= 2, g < nz - 2
    low_y, high_y = h >= 1, h < ny - 1
    part_low = part == 0
    early_to, forward_to = g - 2 + 4 * part, g + 2 - 4 * part
    can_early = jnp.logical_or(jnp.logical_and(part_low, low_z), jnp.logical_and(jnp.logical_not(part_low), high_z))
    can_forward = jnp.logical_or(jnp.logical_and(part_low, high_z), jnp.logical_and(jnp.logical_not(part_low), low_z))
    begin = {
        "here": planes * (1 + part), "there": planes * (2 - part),
        "early": 3 * planes * other, "forward": 3 * planes * part,
    }
    regions = ("here", "there", "early", "forward")
    inner = pl.ds(TILE, rows)

    def remote(src, dst, send, recv, gz, gy):
        return pltpu.make_async_remote_copy(
            src_ref=src, dst_ref=dst, send_sem=send, recv_sem=recv,
            device_id={"gz": gz, "gy": gy}, device_id_type=pl.DeviceIdType.MESH,
        )

    barrier = pltpu.get_barrier_semaphore()
    for d in range(1, nz):
        pl.semaphore_signal(barrier, inc=1, device_id={"gz": lax.rem(g + d, nz), "gy": h}, device_id_type=pl.DeviceIdType.MESH)
    for d in range(1, ny):
        pl.semaphore_signal(barrier, inc=1, device_id={"gz": g, "gy": lax.rem(h + d, ny)}, device_id_type=pl.DeviceIdType.MESH)

    order = [mine] + list(range(mine))

    def body(i):
        return coef if isinstance(i, int) and i == mine else field.at[i]

    def source(i, side):
        return conduct if i == mine else block.at[mine * side + i]

    def local(i):
        return pltpu.make_async_copy(source(i, part), body(i).at[pl.ds(begin["here"], planes), inner], ll.at[i])

    def load(i):
        return pltpu.make_async_copy(source(i, other), outbox.at[i], lo.at[i])

    size = planes // CHUNKS

    def swap(i, k):
        return remote(
            outbox.at[i, pl.ds(k * size, size)], body(i).at[pl.ds(begin["here"] + k * size, size), inner],
            xs.at[i, k], xr.at[i, k], partner, h,
        )

    def swap_in(i, k):
        return remote(
            outbox.at[i, pl.ds(k * size, size)], body(i).at[pl.ds(begin["there"] + k * size, size), inner],
            xs.at[i, k], xr.at[i, k], partner, h,
        )

    def early(i):
        return remote(
            body(i).at[pl.ds(begin["here"], planes), inner], body(i).at[pl.ds(begin["early"], planes), inner],
            es.at[i], er.at[i], early_to, h,
        )

    def forward(i, k):
        return remote(
            body(i).at[pl.ds(begin["there"] + k * size, size), inner],
            body(i).at[pl.ds(begin["forward"] + k * size, size), inner],
            fs.at[i, k], fr.at[i, k], forward_to, h,
        )

    def row_copies(i, q, arriving):
        zs = pl.ds(begin[regions[q]], planes)
        data = body(i)
        down, up = (h + 1, h - 1) if arriving else (h - 1, h + 1)
        ok_down, ok_up = (high_y, low_y) if arriving else (low_y, high_y)
        return [
            (ok_down, remote(data.at[zs, pl.ds(TILE, TILE)], data.at[zs, pl.ds(TILE + rows, TILE)], ys.at[i, q, 0], yr.at[i, q, 0], g, down)),
            (ok_up, remote(data.at[zs, pl.ds(rows, TILE)], data.at[zs, pl.ds(0, TILE)], ys.at[i, q, 1], yr.at[i, q, 1], g, up)),
        ]

    exists = {0: None, 1: None, 2: can_forward, 3: can_early}

    def rows_do(i, q, what, arriving=False):
        for ok, copy in row_copies(i, q, arriving):
            if exists[q] is not None:
                ok = jnp.logical_and(ok, exists[q])
            pl.when(ok)(getattr(copy, what))

    for i in order:
        load(i).start()
    for i in order:
        local(i).start()

    blank = jnp.zeros((tall, columns), jnp.float32)
    edge = jnp.zeros((TILE, columns), jnp.float32)
    for name, exist in (("early", can_forward), ("forward", can_early)):
        @pl.when(jnp.logical_not(exist))
        def _():
            for i in order:
                @pl.loop(0, planes)
                def _(z):
                    body(i)[begin[name] + z] = blank
    for at, exist in ((0, low_y), (TILE + rows, high_y)):
        @pl.when(jnp.logical_not(exist))
        def _():
            for i in order:
                @pl.loop(0, span)
                def _(z):
                    body(i)[z, at : at + TILE, :] = edge

    pl.semaphore_wait(barrier, nz + ny - 2)
    for i in order:
        load(i).wait()
        for k in range(CHUNKS):
            swap(i, k).start()
    for i in order:
        local(i).wait()
        pl.when(can_early)(early(i).start)
        rows_do(i, 0, "start")

    def take(i, k):
        swap_in(i, k).wait_recv()
        pl.when(can_forward)(forward(i, k).start)
        if k == CHUNKS - 1:
            rows_do(i, 1, "start")

    def take_early(i):
        pl.when(can_forward)(early(i).wait_recv)
        rows_do(i, 2, "start")

    def take_forward(i):
        for k in range(CHUNKS):
            pl.when(can_early)(forward(i, k).wait_recv)
        rows_do(i, 3, "start")

    def ready(i):
        for q in range(4):
            rows_do(i, q, "wait_recv", True)

    def sent(i):
        for k in range(CHUNKS):
            pl.when(can_forward)(forward(i, k).wait_send)
        pl.when(can_early)(early(i).wait_send)
        for q in range(4):
            rows_do(i, q, "wait_send")

    take(mine, 0)
    take_early(mine)
    for k in range(1, CHUNKS):
        take(mine, k)
    take_early(0)
    take(0, 0)
    take_forward(mine)
    for k in range(1, CHUNKS):
        take(0, k)
    ready(mine)
    weights = (wz, wy, wx, diag)
    weigh(coef, weights, rows, low_y, high_y)

    @pl.when(jnp.logical_not(low_z))
    def _():
        wz[planes - 1] = blank
        diag[planes] = diag[planes] + coef[planes] * (1.0 / half_width)

    @pl.when(jnp.logical_not(high_z))
    def _():
        wz[3 * planes - 1] = blank
        diag[3 * planes - 1] = diag[3 * planes - 1] + coef[3 * planes - 1] * (1.0 / half_width)

    events = {}

    def plan(v, step, *acts):
        events.setdefault((v, step), []).extend(acts)

    if mine > 1:
        plan(0, 0, lambda: take_early(1), lambda: take(1, 0))
    plan(0, 0, lambda: take_forward(0))
    if mine > 1:
        plan(0, 0, *[functools.partial(take, 1, k) for k in range(1, CHUNKS)])
    for v in range(1, mine):
        if v + 1 < mine:
            plan(v - 1, 2, functools.partial(take_early, v + 1), functools.partial(take, v + 1, 0))
        plan(v - 1, 5, functools.partial(take_forward, v))
        if v + 1 < mine:
            plan(v - 1, 5, *[functools.partial(take, v + 1, k) for k in range(1, CHUNKS)])

    def give_back(v):
        return remote(
            field.at[v, pl.ds(begin["there"], planes), inner], gathered.at[mine * part + v],
            rs.at[v], rr.at[v], partner, h,
        )

    def returned(v):
        return remote(
            field.at[v, pl.ds(begin["there"], planes), inner], gathered.at[mine * other + v],
            rs.at[v], rr.at[v], partner, h,
        )

    def keep(v):
        return pltpu.make_async_copy(
            field.at[v, pl.ds(begin["here"], planes), inner], gathered.at[mine * part + v], rl.at[v]
        )

    @pl.loop(0, mine)
    def _(v):
        plan = steps_of(field.at[v], even, odd)
        for step in range(STEPS + 1):
            if step:
                advance(*plan[step - 1], weights, step)
            for w in range(mine):
                if (w, step) in events:
                    @pl.when(v == w)
                    def _():
                        for act in events[w, step]:
                            act()
            if step == 0:
                ready(v)
            if step == STEPS - 1:
                sent(v)
        give_back(v).start()
        keep(v).start()

    for v in range(mine):
        keep(v).wait()
        returned(v).wait_recv()
    to_out = pltpu.make_async_copy(gathered, filtered, outs)
    to_out.start()

    index = [(i, j) for i in range(vectors) for j in range(i + 1)]
    tiles = rows // 8

    def gram_body(t, accs):
        z, r = t // tiles, pl.multiple_of((t % tiles) * 8, 8)
        accs = list(accs)
        for c in range(columns // 128):
            vals = [gathered[v, z, pl.ds(r, 8), c * 128 : (c + 1) * 128] for v in range(vectors)]
            for p, (i, j) in enumerate(index):
                accs[p] = accs[p] + vals[i] * vals[j]
        return tuple(accs)

    accs = lax.fori_loop(0, planes * tiles, gram_body, tuple(jnp.zeros((8, 128), jnp.float32) for _ in index))
    pairs[...] = jnp.zeros((128, 128), jnp.float32)
    for p, (i, j) in enumerate(index):
        line = jnp.sum(accs[p], axis=0, keepdims=True)
        pairs[i * vectors + j : i * vectors + j + 1, :] = line
        if i != j:
            pairs[j * vectors + i : j * vectors + i + 1, :] = line
    ones = jnp.ones((8, 128), jnp.float32)
    part_sum = lax.dot_general(
        ones, pairs[...], (((1,), (1,)), ((), ())), precision=lax.Precision.HIGHEST,
        preferred_element_type=jnp.float32,
    )

    def total_of(value, slots, send, recv, axis, me, count):
        slots[me] = value
        copies = []
        for d in range(1, count):
            target = lax.rem(me + d, count)
            gz, gy = (target, h) if axis == "gz" else (g, target)
            copy = remote(slots.at[me], slots.at[me], send.at[d - 1], recv.at[d - 1], gz, gy)
            copy.start()
            copies.append(copy)
        for d in range(1, count):
            source = lax.rem(me - d + count, count)
            gz, gy = (source, h) if axis == "gz" else (g, source)
            remote(slots.at[source], slots.at[source], send.at[d - 1], recv.at[d - 1], gz, gy).wait_recv()
        result = slots[0]
        for d in range(1, count):
            result = result + slots[d]
        for copy in copies:
            copy.wait_send()
        return result

    slab = total_of(part_sum, gsum_y, gys, gyr, "gy", h, ny)
    gram_out[...] = total_of(slab, gsum_z, gzs, gzr, "gz", g, nz)

    sent(mine)
    for i in order:
        for k in range(CHUNKS):
            swap(i, k).wait_send()
    for v in range(mine):
        give_back(v).wait_send()
    to_out.wait()


def filter_and_gram(block, conduct):
    nz, ny = lax.axis_size("gz"), lax.axis_size("gy")
    vectors, planes, rows, columns = block.shape
    mine, span, tall = vectors // 2, 4 * planes, rows + 2 * TILE
    f32 = jnp.float32
    dma = pltpu.SemaphoreType.DMA
    volume = pltpu.VMEM((span, tall, columns), f32)
    return pl.pallas_call(
        functools.partial(kernel, nz, ny),
        out_shape=[jax.ShapeDtypeStruct(block.shape, f32), jax.ShapeDtypeStruct((8, 128), f32)],
        in_specs=[pl.BlockSpec(memory_space=pl.ANY)] * 2,
        out_specs=[pl.BlockSpec(memory_space=pl.ANY), pl.BlockSpec(memory_space=pltpu.VMEM)],
        scratch_shapes=[
            pltpu.VMEM((mine, span, tall, columns), f32),
            volume, volume, volume, volume, volume, volume, volume,
            pltpu.VMEM((vectors, planes, rows, columns), f32),
            pltpu.VMEM((128, 128), f32),
            pltpu.VMEM((ny, 8, 128), f32),
            pltpu.VMEM((nz, 8, 128), f32),
            pltpu.VMEM((mine + 1, planes, rows, columns), f32),
            dma((mine + 1,)), dma((mine + 1,)),
            dma((mine + 1, CHUNKS)), dma((mine + 1, CHUNKS)),
            dma((mine + 1,)), dma((mine + 1,)),
            dma((mine + 1, CHUNKS)), dma((mine + 1, CHUNKS)),
            dma((mine + 1, 4, 2)), dma((mine + 1, 4, 2)),
            dma((mine,)), dma((mine,)), dma((mine,)),
            dma((ny,)), dma((ny,)), dma((nz,)), dma((nz,)),
            dma,
        ],
        compiler_params=pltpu.CompilerParams(
            collective_id=0, has_side_effects=True, vmem_limit_bytes=60 * 1024 * 1024
        ),
        name="filter_and_gram",
    )(block, conduct)


def finish_kernel(cells, sums, field, basis, held, result, taken, given):
    vectors, planes, rows, columns = field.shape
    take = [pltpu.make_async_copy(field.at[:, z], held.at[:, z], taken.at[z]) for z in range(planes)]
    give = [pltpu.make_async_copy(result.at[:, z], basis.at[:, z], given.at[z]) for z in range(planes)]
    for z in range(planes):
        take[z].start()
    gram = sums[...]
    low = {}
    factors = {}
    recip = []
    for j in range(vectors):
        for i in range(j, vectors):
            at = i * vectors + j
            value = jnp.broadcast_to(gram[:, at : at + 1], (8, 128))
            for k in range(j):
                value = value - low[i, k] * low[j, k]
            if i == j:
                low[j, j] = jnp.sqrt(value)
                recip.append(1.0 / low[j, j])
            else:
                low[i, j] = value * recip[j]
    for j in range(vectors):
        column = {j: recip[j]}
        for i in range(j + 1, vectors):
            value = low[i, j] * column[j]
            for k in range(j + 1, i):
                value = value + low[i, k] * column[k]
            column[i] = -value * recip[i]
        for i in range(j, vectors):
            factors[i, j] = column[i] * math.sqrt(cells)

    for z in range(planes):
        take[z].wait()

        @pl.loop(0, rows, step=8)
        def _(r):
            r = pl.multiple_of(r, 8)
            for c in range(0, columns, 128):
                vals = [held[v, z, pl.ds(r, 8), c : c + 128] for v in range(vectors)]
                for i in range(vectors):
                    total = factors[i, 0] * vals[0]
                    for j in range(1, i + 1):
                        total = total + factors[i, j] * vals[j]
                    result[i, z, pl.ds(r, 8), c : c + 128] = total

        give[z].start()
    for z in range(planes):
        give[z].wait()


def shards(block, conduct):
    vectors, planes, rows, columns = block.shape
    field, sums = filter_and_gram(block, conduct)
    total_cells = columns * rows * planes * lax.axis_size("gz") * lax.axis_size("gy")
    whole = pltpu.VMEM(block.shape, jnp.float32)
    return pl.pallas_call(
        functools.partial(finish_kernel, total_cells),
        out_shape=jax.ShapeDtypeStruct(block.shape, jnp.float32),
        in_specs=[pl.BlockSpec(memory_space=pltpu.VMEM), pl.BlockSpec(memory_space=pl.ANY)],
        out_specs=pl.BlockSpec(memory_space=pl.ANY),
        scratch_shapes=[whole, whole, pltpu.SemaphoreType.DMA((planes,)), pltpu.SemaphoreType.DMA((planes,))],
        compiler_params=pltpu.CompilerParams(vmem_limit_bytes=60 * 1024 * 1024),
        name="finish",
    )(sums, field)


def solution(mesh):
    in_specs = (P(None, "gz", "gy", None), P("gz", "gy", None))
    out_specs = P(None, "gz", "gy", None)
    return jax.shard_map(shards, mesh=mesh, in_specs=in_specs, out_specs=out_specs, check_vma=False)
```

```python
import functools
import math

import jax
import jax.numpy as jnp
from jax import lax
from jax.experimental import pallas as pl
from jax.experimental.pallas import tpu as pltpu
from jax.sharding import PartitionSpec as P

DEG = 4
PASSES = 2
STEPS = DEG * PASSES
CHUNKS = 4
ARRIVES = (1, 2, 4, 6)
TILE = 8

mid_point = 12.75
half_width = 11.25


def weigh(coef, weights, rows, low_y, high_y):
    wz, wy, wx, diag = weights
    span, tall, columns = coef.shape
    scale = 1.0 / half_width
    row_id = lax.broadcasted_iota(jnp.int32, (tall, columns), 0)
    col_id = lax.broadcasted_iota(jnp.int32, (tall, columns), 1)
    cut = ((row_id == TILE + rows - 1) & jnp.logical_not(high_y)) | ((row_id == TILE - 1) & jnp.logical_not(low_y))
    first, last = col_id == 0, col_id == columns - 1
    wz[0] = scale * (coef[0] + coef[1])

    @pl.loop(1, span - 1, unroll=2)
    def _(z):
        plane = scale * coef[z]
        yp = plane + pltpu.roll(plane, tall - 1, 0)
        ym = plane + pltpu.roll(plane, 1, 0)
        xp = plane + jnp.where(last, 0.0, pltpu.roll(plane, columns - 1, 1))
        xm = plane + jnp.where(first, 0.0, pltpu.roll(plane, 1, 1))
        wz[z] = plane + scale * coef[z + 1]
        wx[z] = jnp.where(last, 0.0, xp)
        wy[z] = jnp.where(cut, 0.0, yp)
        diag[z] = (yp + ym) + (xp + xm) - 2.0 * mid_point / half_width


def advance(now, prev, dst, weights, step):
    wz, wy, wx, diag = weights
    span, tall, columns = now.shape
    own, wide = tall // TILE - 2, columns // 128
    row_id = lax.broadcasted_iota(jnp.int32, (TILE, 128), 0)
    col_id = lax.broadcasted_iota(jnp.int32, (TILE, 128), 1)
    top, bottom, start, end = row_id == 0, row_id == TILE - 1, col_id == 0, col_id == 127

    def at(ref, z, r, c):
        return ref[z, r * TILE : (r + 1) * TILE, c * 128 : (c + 1) * 128]

    def sweep(tiles, low, high):
        parts = [(r, c) for r, _, _ in tiles for c in range(wide)]
        current = {t: at(now, low, *t) for t in parts}
        flux = {t: at(wz, low - 1, *t) * (current[t] - at(now, low - 1, *t)) for t in parts}
        for z in range(low, high):
            further = {t: at(now, z + 1, *t) for t in parts}
            weight = {t: at(wy, z, *t) for t in parts}
            product = {t: weight[t] * current[t] for t in parts}
            for r, smaller, larger in tiles:
                across = [at(wx, z, r, c) for c in range(wide)]
                lefts = [pltpu.roll(across[c] * current[r, c], 1, 1) for c in range(wide)]
                rights = [pltpu.roll(current[r, c], 127, 1) for c in range(wide)]
                for c in range(wide):
                    t = (r, c)
                    mid = current[t]
                    below = product[t] if smaller is None else product.get((smaller, c))
                    if below is None:
                        below = at(wy, z, smaller, c) * at(now, z, smaller, c)
                    above = mid if larger is None else current.get((larger, c))
                    if above is None:
                        above = at(now, z, larger, c)
                    below = pltpu.roll(jnp.where(bottom, below, product[t]), 1, 0)
                    above = pltpu.roll(jnp.where(top, above, mid), TILE - 1, 0)
                    left = jnp.where(start, lefts[(c - 1) % wide], lefts[c])
                    right = jnp.where(end, rights[(c + 1) % wide], rights[c])
                    onward = at(wz, z, *t) * (further[t] - mid)
                    total = at(diag, z, *t) * mid + (flux[t] - onward)
                    total = total - (below + weight[t] * above)
                    total = total - (left + across[c] * right)
                    if prev is None:
                        total = 0.5 * total
                    else:
                        total = total - at(prev, z, *t)
                    dst[z, r * TILE : (r + 1) * TILE, c * 128 : (c + 1) * 128] = total
                    flux[t] = onward
            current = further

    for r in range(1, own + 1, 4):
        sweep([(q, q - 1, q + 1) for q in range(r, min(r + 4, own + 1))], step, span - step)
    if step < STEPS:
        sweep([(0, None, 1), (own + 1, own, None)], step + 1, span - step - 1)


def steps_of(field, even, odd):
    held = [field]
    plan = []
    for step in range(1, STEPS + 1):
        dst = field if step == STEPS else (odd if step % 2 else even)
        first = step % DEG == 1
        plan.append((held[-1], None if first else held[-2], dst))
        held.append(dst)
    return plan


def kernel(
    nz, ny,
    block, conduct, gathered, gram_out,
    field, even, odd, coef, wz, wy, wx, diag,
    pairs, gsum_y, gsum_z,
    outbox,
    lo, ll, xs, xr, es, er, fs, fr, ys, yr, rs, rr, rl, gys, gyr, gzs, gzr,
):
    g = lax.axis_index("gz")
    h = lax.axis_index("gy")
    part = lax.rem(g, 2)
    other = 1 - part
    partner = g + 1 - 2 * part
    vectors, planes, rows, columns = block.shape
    mine = vectors // 2
    span, tall = 4 * planes, rows + 2 * TILE
    low_z, high_z = g >= 2, g < nz - 2
    low_y, high_y = h >= 1, h < ny - 1
    part_low = part == 0
    early_to, forward_to = g - 2 + 4 * part, g + 2 - 4 * part
    can_early = jnp.logical_or(jnp.logical_and(part_low, low_z), jnp.logical_and(jnp.logical_not(part_low), high_z))
    can_forward = jnp.logical_or(jnp.logical_and(part_low, high_z), jnp.logical_and(jnp.logical_not(part_low), low_z))
    begin = {
        "here": planes * (1 + part), "there": planes * (2 - part),
        "early": 3 * planes * other, "forward": 3 * planes * part,
    }
    regions = ("here", "there", "early", "forward")
    inner = pl.ds(TILE, rows)

    def remote(src, dst, send, recv, gz, gy):
        return pltpu.make_async_remote_copy(
            src_ref=src, dst_ref=dst, send_sem=send, recv_sem=recv,
            device_id={"gz": gz, "gy": gy}, device_id_type=pl.DeviceIdType.MESH,
        )

    barrier = pltpu.get_barrier_semaphore()
    for d in range(1, nz):
        pl.semaphore_signal(barrier, inc=1, device_id={"gz": lax.rem(g + d, nz), "gy": h}, device_id_type=pl.DeviceIdType.MESH)
    for d in range(1, ny):
        pl.semaphore_signal(barrier, inc=1, device_id={"gz": g, "gy": lax.rem(h + d, ny)}, device_id_type=pl.DeviceIdType.MESH)

    order = [mine] + list(range(mine))

    def body(i):
        return coef if isinstance(i, int) and i == mine else field.at[i]

    def source(i, side):
        return conduct if i == mine else block.at[mine * side + i]

    def local(i):
        return pltpu.make_async_copy(source(i, part), body(i).at[pl.ds(begin["here"], planes), inner], ll.at[i])

    def load(i):
        return pltpu.make_async_copy(source(i, other), outbox.at[i], lo.at[i])

    size = planes // CHUNKS

    def swap(i, k):
        return remote(
            outbox.at[i, pl.ds(k * size, size)], body(i).at[pl.ds(begin["here"] + k * size, size), inner],
            xs.at[i, k], xr.at[i, k], partner, h,
        )

    def swap_in(i, k):
        return remote(
            outbox.at[i, pl.ds(k * size, size)], body(i).at[pl.ds(begin["there"] + k * size, size), inner],
            xs.at[i, k], xr.at[i, k], partner, h,
        )

    def early(i):
        return remote(
            body(i).at[pl.ds(begin["here"], planes), inner], body(i).at[pl.ds(begin["early"], planes), inner],
            es.at[i], er.at[i], early_to, h,
        )

    def forward(i, k):
        return remote(
            body(i).at[pl.ds(begin["there"] + k * size, size), inner],
            body(i).at[pl.ds(begin["forward"] + k * size, size), inner],
            fs.at[i, k], fr.at[i, k], forward_to, h,
        )

    def row_copies(i, q, arriving):
        zs = pl.ds(begin[regions[q]], planes)
        data = body(i)
        down, up = (h + 1, h - 1) if arriving else (h - 1, h + 1)
        ok_down, ok_up = (high_y, low_y) if arriving else (low_y, high_y)
        return [
            (ok_down, remote(data.at[zs, pl.ds(TILE, TILE)], data.at[zs, pl.ds(TILE + rows, TILE)], ys.at[i, q, 0], yr.at[i, q, 0], g, down)),
            (ok_up, remote(data.at[zs, pl.ds(rows, TILE)], data.at[zs, pl.ds(0, TILE)], ys.at[i, q, 1], yr.at[i, q, 1], g, up)),
        ]

    exists = {0: None, 1: None, 2: can_forward, 3: can_early}

    def rows_do(i, q, what, arriving=False):
        for ok, copy in row_copies(i, q, arriving):
            if exists[q] is not None:
                ok = jnp.logical_and(ok, exists[q])
            pl.when(ok)(getattr(copy, what))

    for i in order:
        load(i).start()
    for i in order:
        local(i).start()

    blank = jnp.zeros((tall, columns), jnp.float32)
    edge = jnp.zeros((TILE, columns), jnp.float32)
    for name, exist in (("early", can_forward), ("forward", can_early)):
        @pl.when(jnp.logical_not(exist))
        def _():
            for i in order:
                @pl.loop(0, planes)
                def _(z):
                    body(i)[begin[name] + z] = blank
    for at, exist in ((0, low_y), (TILE + rows, high_y)):
        @pl.when(jnp.logical_not(exist))
        def _():
            for i in order:
                @pl.loop(0, span)
                def _(z):
                    body(i)[z, at : at + TILE, :] = edge

    pl.semaphore_wait(barrier, nz + ny - 2)
    for i in order:
        load(i).wait()
        for k in range(CHUNKS):
            swap(i, k).start()
    for i in order:
        local(i).wait()
        pl.when(can_early)(early(i).start)
        rows_do(i, 0, "start")

    def take(i, k):
        swap_in(i, k).wait_recv()
        pl.when(can_forward)(forward(i, k).start)
        if k == CHUNKS - 1:
            rows_do(i, 1, "start")

    def take_early(i):
        pl.when(can_forward)(early(i).wait_recv)
        rows_do(i, 2, "start")

    def take_forward(i):
        for k in range(CHUNKS):
            pl.when(can_early)(forward(i, k).wait_recv)
        rows_do(i, 3, "start")

    def ready(i):
        for q in range(4):
            rows_do(i, q, "wait_recv", True)

    def sent(i):
        for k in range(CHUNKS):
            pl.when(can_forward)(forward(i, k).wait_send)
        pl.when(can_early)(early(i).wait_send)
        for q in range(4):
            rows_do(i, q, "wait_send")

    take(mine, 0)
    take_early(mine)
    for k in range(1, CHUNKS):
        take(mine, k)
    take_early(0)
    half = CHUNKS // 2
    for k in range(half):
        take(0, k)
    take_forward(mine)
    for k in range(half, CHUNKS):
        take(0, k)
    ready(mine)
    if mine > 1:
        take_early(1)
        take(1, 0)
    weights = (wz, wy, wx, diag)
    weigh(coef, weights, rows, low_y, high_y)

    @pl.when(jnp.logical_not(low_z))
    def _():
        wz[planes - 1] = blank
        diag[planes] = diag[planes] + coef[planes] * (1.0 / half_width)

    @pl.when(jnp.logical_not(high_z))
    def _():
        wz[3 * planes - 1] = blank
        diag[3 * planes - 1] = diag[3 * planes - 1] + coef[3 * planes - 1] * (1.0 / half_width)

    events = {}

    def plan(v, step, *acts):
        events.setdefault((v, step), []).extend(acts)

    if mine > 1:
        plan(0, 0, functools.partial(take, 1, 1), lambda: take_forward(0))
        plan(0, 0, *[functools.partial(take, 1, k) for k in range(2, CHUNKS)])
    else:
        plan(0, 0, lambda: take_forward(0))
    for v in range(1, mine):
        if v + 1 < mine:
            plan(v - 1, ARRIVES[0], functools.partial(take_early, v + 1))
            for k in range(CHUNKS):
                plan(v - 1, ARRIVES[k], functools.partial(take, v + 1, k))
        plan(v - 1, 3, functools.partial(take_forward, v))

    def give_back(v):
        return remote(
            field.at[v, pl.ds(begin["there"], planes), inner], gathered.at[mine * part + v],
            rs.at[v], rr.at[v], partner, h,
        )

    def returned(v):
        return remote(
            field.at[v, pl.ds(begin["there"], planes), inner], gathered.at[mine * other + v],
            rs.at[v], rr.at[v], partner, h,
        )

    def keep(v):
        return pltpu.make_async_copy(
            field.at[v, pl.ds(begin["here"], planes), inner], gathered.at[mine * part + v], rl.at[v]
        )

    @pl.loop(0, mine)
    def _(v):
        plan = steps_of(field.at[v], even, odd)
        for step in range(STEPS + 1):
            if step:
                advance(*plan[step - 1], weights, step)
            for w in range(mine):
                if (w, step) in events:
                    @pl.when(v == w)
                    def _():
                        for act in events[w, step]:
                            act()
            if step == 0:
                ready(v)
            if step == STEPS - 1:
                sent(v)
        give_back(v).start()
        keep(v).start()

    index = [(i, j) for i in range(vectors) for j in range(i + 1)]
    last = (mine - 1, vectors - 1)
    tiles = rows // 8
    sums = {}

    def add_products(chosen):
        used = sorted({i for pair in chosen for i in pair})

        def gram_body(t, accs):
            z, r = t // tiles, pl.multiple_of((t % tiles) * 8, 8)
            accs = list(accs)
            for c in range(columns // 128):
                vals = {v: gathered[v, z, pl.ds(r, 8), c * 128 : (c + 1) * 128] for v in used}
                for p, (i, j) in enumerate(chosen):
                    accs[p] = accs[p] + vals[i] * vals[j]
            return tuple(accs)

        zeros = tuple(jnp.zeros((8, 128), jnp.float32) for _ in chosen)
        sums.update(zip(chosen, lax.fori_loop(0, planes * tiles, gram_body, zeros, unroll=2)))

    for v in range(mine):
        if v == mine - 1:
            early_pairs = [p for p in index if not set(p) & set(last)]
            if early_pairs:
                add_products(early_pairs)
        keep(v).wait()
        returned(v).wait_recv()
    add_products([p for p in index if set(p) & set(last)])
    accs = [sums[p] for p in index]
    pairs[...] = jnp.zeros((128, 128), jnp.float32)
    for p, (i, j) in enumerate(index):
        line = jnp.sum(accs[p], axis=0, keepdims=True)
        pairs[i * vectors + j : i * vectors + j + 1, :] = line
        if i != j:
            pairs[j * vectors + i : j * vectors + i + 1, :] = line
    ones = jnp.ones((8, 128), jnp.float32)
    part_sum = lax.dot_general(
        ones, pairs[...], (((1,), (1,)), ((), ())), precision=lax.Precision.HIGHEST,
        preferred_element_type=jnp.float32,
    )

    def total_of(value, slots, send, recv, axis, me, count):
        slots[me] = value
        copies = []
        for d in range(1, count):
            target = lax.rem(me + d, count)
            gz, gy = (target, h) if axis == "gz" else (g, target)
            copy = remote(slots.at[me], slots.at[me], send.at[d - 1], recv.at[d - 1], gz, gy)
            copy.start()
            copies.append(copy)
        for d in range(1, count):
            source = lax.rem(me - d + count, count)
            gz, gy = (source, h) if axis == "gz" else (g, source)
            remote(slots.at[source], slots.at[source], send.at[d - 1], recv.at[d - 1], gz, gy).wait_recv()
        result = slots[0]
        for d in range(1, count):
            result = result + slots[d]
        for copy in copies:
            copy.wait_send()
        return result

    slab = total_of(part_sum, gsum_y, gys, gyr, "gy", h, ny)
    gram_out[...] = total_of(slab, gsum_z, gzs, gzr, "gz", g, nz)

    sent(mine)
    for i in order:
        for k in range(CHUNKS):
            swap(i, k).wait_send()
    for v in range(mine):
        give_back(v).wait_send()


def filter_and_gram(block, conduct):
    nz, ny = lax.axis_size("gz"), lax.axis_size("gy")
    vectors, planes, rows, columns = block.shape
    mine, span, tall = vectors // 2, 4 * planes, rows + 2 * TILE
    f32 = jnp.float32
    dma = pltpu.SemaphoreType.DMA
    volume = pltpu.VMEM((span, tall, columns), f32)
    return pl.pallas_call(
        functools.partial(kernel, nz, ny),
        out_shape=[jax.ShapeDtypeStruct(block.shape, f32), jax.ShapeDtypeStruct((8, 128), f32)],
        in_specs=[pl.BlockSpec(memory_space=pltpu.HBM)] * 2,
        out_specs=[pl.BlockSpec(memory_space=pltpu.VMEM)] * 2,
        scratch_shapes=[
            pltpu.VMEM((mine, span, tall, columns), f32),
            volume, volume, volume, volume, volume, volume, volume,
            pltpu.VMEM((128, 128), f32),
            pltpu.VMEM((ny, 8, 128), f32),
            pltpu.VMEM((nz, 8, 128), f32),
            pltpu.VMEM((mine + 1, planes, rows, columns), f32),
            dma((mine + 1,)), dma((mine + 1,)),
            dma((mine + 1, CHUNKS)), dma((mine + 1, CHUNKS)),
            dma((mine + 1,)), dma((mine + 1,)),
            dma((mine + 1, CHUNKS)), dma((mine + 1, CHUNKS)),
            dma((mine + 1, 4, 2)), dma((mine + 1, 4, 2)),
            dma((mine,)), dma((mine,)), dma((mine,)),
            dma((ny,)), dma((ny,)), dma((nz,)), dma((nz,)),
        ],
        compiler_params=pltpu.CompilerParams(
            collective_id=0, has_side_effects=True, vmem_limit_bytes=51 * 1024 * 1024
        ),
        name="filter_and_gram",
    )(block, conduct)


def finish_kernel(cells, sums, held, basis, result, given):
    vectors, planes, rows, columns = held.shape
    give = [pltpu.make_async_copy(result.at[:, z], basis.at[:, z], given.at[z]) for z in range(planes)]
    gram = sums[...]
    low = {}
    factors = {}
    recip = []
    for j in range(vectors):
        for i in range(j, vectors):
            at = i * vectors + j
            value = jnp.broadcast_to(gram[:, at : at + 1], (8, 128))
            for k in range(j):
                value = value - low[i, k] * low[j, k]
            if i == j:
                low[j, j] = jnp.sqrt(value)
                recip.append(1.0 / low[j, j])
            else:
                low[i, j] = value * recip[j]
    for j in range(vectors):
        column = {j: recip[j]}
        for i in range(j + 1, vectors):
            value = low[i, j] * column[j]
            for k in range(j + 1, i):
                value = value + low[i, k] * column[k]
            column[i] = -value * recip[i]
        for i in range(j, vectors):
            factors[i, j] = column[i] * math.sqrt(cells)

    for z in range(planes):
        @pl.loop(0, rows, step=8)
        def _(r):
            r = pl.multiple_of(r, 8)
            for c in range(0, columns, 128):
                vals = [held[v, z, pl.ds(r, 8), c : c + 128] for v in range(vectors)]
                for i in range(vectors):
                    total = factors[i, 0] * vals[0]
                    for j in range(1, i + 1):
                        total = total + factors[i, j] * vals[j]
                    result[i, z, pl.ds(r, 8), c : c + 128] = total

        give[z].start()
    for z in range(planes):
        give[z].wait()


def shards(block, conduct):
    vectors, planes, rows, columns = block.shape
    field, sums = filter_and_gram(block, conduct)
    total_cells = columns * rows * planes * lax.axis_size("gz") * lax.axis_size("gy")
    return pl.pallas_call(
        functools.partial(finish_kernel, total_cells),
        out_shape=jax.ShapeDtypeStruct(block.shape, jnp.float32),
        in_specs=[pl.BlockSpec(memory_space=pltpu.VMEM)] * 2,
        out_specs=pl.BlockSpec(memory_space=pltpu.HBM),
        scratch_shapes=[pltpu.VMEM(block.shape, jnp.float32), pltpu.SemaphoreType.DMA((planes,))],
        compiler_params=pltpu.CompilerParams(vmem_limit_bytes=40 * 1024 * 1024),
        name="finish",
    )(sums, field)


def solution(mesh):
    in_specs = (P(None, "gz", "gy", None), P("gz", "gy", None))
    out_specs = P(None, "gz", "gy", None)
    return jax.shard_map(shards, mesh=mesh, in_specs=in_specs, out_specs=out_specs, check_vma=False)
```

```python
import functools
import math

import jax
import jax.numpy as jnp
from jax import lax
from jax.experimental import pallas as pl
from jax.experimental.pallas import tpu as pltpu
from jax.sharding import PartitionSpec as P

DEG = 4
PASSES = 2
STEPS = DEG * PASSES
CHUNKS = 4
DIRECT = 32
ARRIVES = (1, 2, 4, 6)
TILE = 8

mid_point = 12.75
half_width = 11.25


def weigh(coef, weights, rows, low_y, high_y):
    wz, wy, wx, diag = weights
    span, tall, columns = coef.shape
    scale = 1.0 / half_width
    row_id = lax.broadcasted_iota(jnp.int32, (tall, columns), 0)
    col_id = lax.broadcasted_iota(jnp.int32, (tall, columns), 1)
    cut = ((row_id == TILE + rows - 1) & jnp.logical_not(high_y)) | ((row_id == TILE - 1) & jnp.logical_not(low_y))
    first, last = col_id == 0, col_id == columns - 1
    wz[0] = scale * (coef[0] + coef[1])

    @pl.loop(1, span - 1, unroll=2)
    def _(z):
        plane = scale * coef[z]
        yp = plane + pltpu.roll(plane, tall - 1, 0)
        ym = plane + pltpu.roll(plane, 1, 0)
        xp = plane + jnp.where(last, 0.0, pltpu.roll(plane, columns - 1, 1))
        xm = plane + jnp.where(first, 0.0, pltpu.roll(plane, 1, 1))
        wz[z] = plane + scale * coef[z + 1]
        wx[z] = jnp.where(last, 0.0, xp)
        wy[z] = jnp.where(cut, 0.0, yp)
        diag[z] = (yp + ym) + (xp + xm) - 2.0 * mid_point / half_width


def advance(now, prev, dst, weights, step):
    wz, wy, wx, diag = weights
    span, tall, columns = now.shape
    own, wide = tall // TILE - 2, columns // 128
    row_id = lax.broadcasted_iota(jnp.int32, (TILE, 128), 0)
    col_id = lax.broadcasted_iota(jnp.int32, (TILE, 128), 1)
    top, bottom, start, end = row_id == 0, row_id == TILE - 1, col_id == 0, col_id == 127

    def at(ref, z, r, c):
        return ref[z, r * TILE : (r + 1) * TILE, c * 128 : (c + 1) * 128]

    def sweep(tiles, low, high):
        parts = [(r, c) for r, _, _ in tiles for c in range(wide)]
        current = {t: at(now, low, *t) for t in parts}
        flux = {t: at(wz, low - 1, *t) * (current[t] - at(now, low - 1, *t)) for t in parts}
        for z in range(low, high):
            further = {t: at(now, z + 1, *t) for t in parts}
            weight = {t: at(wy, z, *t) for t in parts}
            product = {t: weight[t] * current[t] for t in parts}
            for r, smaller, larger in tiles:
                across = [at(wx, z, r, c) for c in range(wide)]
                lefts = [pltpu.roll(across[c] * current[r, c], 1, 1) for c in range(wide)]
                rights = [pltpu.roll(current[r, c], 127, 1) for c in range(wide)]
                for c in range(wide):
                    t = (r, c)
                    mid = current[t]
                    below = product[t] if smaller is None else product.get((smaller, c))
                    if below is None:
                        below = at(wy, z, smaller, c) * at(now, z, smaller, c)
                    above = mid if larger is None else current.get((larger, c))
                    if above is None:
                        above = at(now, z, larger, c)
                    below = pltpu.roll(jnp.where(bottom, below, product[t]), 1, 0)
                    above = pltpu.roll(jnp.where(top, above, mid), TILE - 1, 0)
                    left = jnp.where(start, lefts[(c - 1) % wide], lefts[c])
                    right = jnp.where(end, rights[(c + 1) % wide], rights[c])
                    onward = at(wz, z, *t) * (further[t] - mid)
                    total = at(diag, z, *t) * mid + (flux[t] - onward)
                    total = total - (below + weight[t] * above)
                    total = total - (left + across[c] * right)
                    if prev is None:
                        total = 0.5 * total
                    else:
                        total = total - at(prev, z, *t)
                    dst[z, r * TILE : (r + 1) * TILE, c * 128 : (c + 1) * 128] = total
                    flux[t] = onward
            current = further

    for r in range(1, own + 1, 4):
        sweep([(q, q - 1, q + 1) for q in range(r, min(r + 4, own + 1))], step, span - step)
    if step < STEPS:
        sweep([(0, None, 1), (own + 1, own, None)], step + 1, span - step - 1)


def steps_of(field, even, odd):
    held = [field]
    plan = []
    for step in range(1, STEPS + 1):
        dst = field if step == STEPS else (odd if step % 2 else even)
        first = step % DEG == 1
        plan.append((held[-1], None if first else held[-2], dst))
        held.append(dst)
    return plan


def kernel(
    nz, ny,
    block, conduct, gathered, gram_out,
    field, even, odd, coef, wz, wy, wx, diag,
    pairs, gsum_y, gsum_z, parts,
    outbox,
    lo, ll, xs, xr, es, er, fs, fr, ys, yr, rs, rr, rl, gys, gyr, gzs, gzr, pas, par,
):
    g = lax.axis_index("gz")
    h = lax.axis_index("gy")
    part = lax.rem(g, 2)
    other = 1 - part
    partner = g + 1 - 2 * part
    vectors, planes, rows, columns = block.shape
    mine = vectors // 2
    span, tall = 4 * planes, rows + 2 * TILE
    low_z, high_z = g >= 2, g < nz - 2
    low_y, high_y = h >= 1, h < ny - 1
    part_low = part == 0
    early_to, forward_to = g - 2 + 4 * part, g + 2 - 4 * part
    can_early = jnp.logical_or(jnp.logical_and(part_low, low_z), jnp.logical_and(jnp.logical_not(part_low), high_z))
    can_forward = jnp.logical_or(jnp.logical_and(part_low, high_z), jnp.logical_and(jnp.logical_not(part_low), low_z))
    begin = {
        "here": planes * (1 + part), "there": planes * (2 - part),
        "early": 3 * planes * other, "forward": 3 * planes * part,
    }
    regions = ("here", "there", "early", "forward")
    inner = pl.ds(TILE, rows)

    def remote(src, dst, send, recv, gz, gy):
        return pltpu.make_async_remote_copy(
            src_ref=src, dst_ref=dst, send_sem=send, recv_sem=recv,
            device_id={"gz": gz, "gy": gy}, device_id_type=pl.DeviceIdType.MESH,
        )

    barrier = pltpu.get_barrier_semaphore()
    count, me = nz * ny, g * ny + h
    direct = count <= DIRECT

    def greet(gz, gy):
        pl.semaphore_signal(barrier, inc=1, device_id={"gz": gz, "gy": gy}, device_id_type=pl.DeviceIdType.MESH)

    def peer(d):
        to = lax.rem(me + d, count)
        return to // ny, lax.rem(to, ny)

    if direct:
        for d in range(1, count):
            greet(*peer(d))
        greeted = count - 1
    else:
        for d in range(1, nz):
            greet(lax.rem(g + d, nz), h)
        for d in range(1, ny):
            greet(g, lax.rem(h + d, ny))
        greeted = nz + ny - 2

    order = [mine] + list(range(mine))

    def body(i):
        return coef if isinstance(i, int) and i == mine else field.at[i]

    def source(i, side):
        return conduct if i == mine else block.at[mine * side + i]

    def local(i):
        return pltpu.make_async_copy(source(i, part), body(i).at[pl.ds(begin["here"], planes), inner], ll.at[i])

    def load(i):
        return pltpu.make_async_copy(source(i, other), outbox.at[i], lo.at[i])

    size = planes // CHUNKS

    def swap(i, k):
        return remote(
            outbox.at[i, pl.ds(k * size, size)], body(i).at[pl.ds(begin["here"] + k * size, size), inner],
            xs.at[i, k], xr.at[i, k], partner, h,
        )

    def swap_in(i, k):
        return remote(
            outbox.at[i, pl.ds(k * size, size)], body(i).at[pl.ds(begin["there"] + k * size, size), inner],
            xs.at[i, k], xr.at[i, k], partner, h,
        )

    def early(i):
        return remote(
            body(i).at[pl.ds(begin["here"], planes), inner], body(i).at[pl.ds(begin["early"], planes), inner],
            es.at[i], er.at[i], early_to, h,
        )

    def forward(i, k):
        return remote(
            body(i).at[pl.ds(begin["there"] + k * size, size), inner],
            body(i).at[pl.ds(begin["forward"] + k * size, size), inner],
            fs.at[i, k], fr.at[i, k], forward_to, h,
        )

    def row_copies(i, q, arriving):
        zs = pl.ds(begin[regions[q]], planes)
        data = body(i)
        down, up = (h + 1, h - 1) if arriving else (h - 1, h + 1)
        ok_down, ok_up = (high_y, low_y) if arriving else (low_y, high_y)
        return [
            (ok_down, remote(data.at[zs, pl.ds(TILE, TILE)], data.at[zs, pl.ds(TILE + rows, TILE)], ys.at[i, q, 0], yr.at[i, q, 0], g, down)),
            (ok_up, remote(data.at[zs, pl.ds(rows, TILE)], data.at[zs, pl.ds(0, TILE)], ys.at[i, q, 1], yr.at[i, q, 1], g, up)),
        ]

    exists = {0: None, 1: None, 2: can_forward, 3: can_early}

    def rows_do(i, q, what, arriving=False):
        for ok, copy in row_copies(i, q, arriving):
            if exists[q] is not None:
                ok = jnp.logical_and(ok, exists[q])
            pl.when(ok)(getattr(copy, what))

    for i in order:
        load(i).start()
    for i in order:
        local(i).start()

    blank = jnp.zeros((tall, columns), jnp.float32)
    edge = jnp.zeros((TILE, columns), jnp.float32)
    for name, exist in (("early", can_forward), ("forward", can_early)):
        @pl.when(jnp.logical_not(exist))
        def _():
            for i in order:
                @pl.loop(0, planes)
                def _(z):
                    body(i)[begin[name] + z] = blank
    for at, exist in ((0, low_y), (TILE + rows, high_y)):
        @pl.when(jnp.logical_not(exist))
        def _():
            for i in order:
                @pl.loop(0, span)
                def _(z):
                    body(i)[z, at : at + TILE, :] = edge

    pl.semaphore_wait(barrier, greeted)
    for i in order:
        load(i).wait()
        for k in range(CHUNKS):
            swap(i, k).start()
    for i in order:
        local(i).wait()
        pl.when(can_early)(early(i).start)
        rows_do(i, 0, "start")

    def take(i, k):
        swap_in(i, k).wait_recv()
        pl.when(can_forward)(forward(i, k).start)
        if k == CHUNKS - 1:
            rows_do(i, 1, "start")

    def take_early(i):
        pl.when(can_forward)(early(i).wait_recv)
        rows_do(i, 2, "start")

    def take_forward(i):
        for k in range(CHUNKS):
            pl.when(can_early)(forward(i, k).wait_recv)
        rows_do(i, 3, "start")

    def ready(i):
        for q in range(4):
            rows_do(i, q, "wait_recv", True)

    def sent(i):
        for k in range(CHUNKS):
            pl.when(can_forward)(forward(i, k).wait_send)
        pl.when(can_early)(early(i).wait_send)
        for q in range(4):
            rows_do(i, q, "wait_send")

    take(mine, 0)
    take_early(mine)
    for k in range(1, CHUNKS):
        take(mine, k)
    take_early(0)
    half = CHUNKS // 2
    for k in range(half):
        take(0, k)
    take_forward(mine)
    for k in range(half, CHUNKS):
        take(0, k)
    ready(mine)
    if mine > 1:
        take_early(1)
        take(1, 0)
    weights = (wz, wy, wx, diag)
    weigh(coef, weights, rows, low_y, high_y)

    @pl.when(jnp.logical_not(low_z))
    def _():
        wz[planes - 1] = blank
        diag[planes] = diag[planes] + coef[planes] * (1.0 / half_width)

    @pl.when(jnp.logical_not(high_z))
    def _():
        wz[3 * planes - 1] = blank
        diag[3 * planes - 1] = diag[3 * planes - 1] + coef[3 * planes - 1] * (1.0 / half_width)

    events = {}

    def plan(v, step, *acts):
        events.setdefault((v, step), []).extend(acts)

    if mine > 1:
        plan(0, 0, functools.partial(take, 1, 1), lambda: take_forward(0))
        plan(0, 0, *[functools.partial(take, 1, k) for k in range(2, CHUNKS)])
    else:
        plan(0, 0, lambda: take_forward(0))
    for v in range(1, mine):
        if v + 1 < mine:
            plan(v - 1, ARRIVES[0], functools.partial(take_early, v + 1))
            for k in range(CHUNKS):
                plan(v - 1, ARRIVES[k], functools.partial(take, v + 1, k))
        plan(v - 1, 3, functools.partial(take_forward, v))

    def give_back(v):
        return remote(
            field.at[v, pl.ds(begin["there"], planes), inner], gathered.at[mine * part + v],
            rs.at[v], rr.at[v], partner, h,
        )

    def returned(v):
        return remote(
            field.at[v, pl.ds(begin["there"], planes), inner], gathered.at[mine * other + v],
            rs.at[v], rr.at[v], partner, h,
        )

    def keep(v):
        return pltpu.make_async_copy(
            field.at[v, pl.ds(begin["here"], planes), inner], gathered.at[mine * part + v], rl.at[v]
        )

    @pl.loop(0, mine)
    def _(v):
        plan = steps_of(field.at[v], even, odd)
        for step in range(STEPS + 1):
            if step:
                advance(*plan[step - 1], weights, step)
            for w in range(mine):
                if (w, step) in events:
                    @pl.when(v == w)
                    def _():
                        for act in events[w, step]:
                            act()
            if step == 0:
                ready(v)
            if step == STEPS - 1:
                sent(v)
        give_back(v).start()
        keep(v).start()

    index = [(i, j) for i in range(vectors) for j in range(i + 1)]
    last = (mine - 1, vectors - 1)
    tiles = rows // 8
    sums = {}

    def add_products(chosen):
        used = sorted({i for pair in chosen for i in pair})

        def gram_body(t, accs):
            z, r = t // tiles, pl.multiple_of((t % tiles) * 8, 8)
            accs = list(accs)
            for c in range(columns // 128):
                vals = {v: gathered[v, z, pl.ds(r, 8), c * 128 : (c + 1) * 128] for v in used}
                for p, (i, j) in enumerate(chosen):
                    accs[p] = accs[p] + vals[i] * vals[j]
            return tuple(accs)

        zeros = tuple(jnp.zeros((8, 128), jnp.float32) for _ in chosen)
        sums.update(zip(chosen, lax.fori_loop(0, planes * tiles, gram_body, zeros, unroll=2)))

    for v in range(mine):
        if v == mine - 1:
            early_pairs = [p for p in index if not set(p) & set(last)]
            if early_pairs:
                add_products(early_pairs)
        keep(v).wait()
        returned(v).wait_recv()
    add_products([p for p in index if set(p) & set(last)])
    accs = [sums[p] for p in index]
    pairs[...] = jnp.zeros((128, 128), jnp.float32)
    for p, (i, j) in enumerate(index):
        line = jnp.sum(accs[p], axis=0, keepdims=True)
        pairs[i * vectors + j : i * vectors + j + 1, :] = line
        if i != j:
            pairs[j * vectors + i : j * vectors + i + 1, :] = line
    ones = jnp.ones((8, 128), jnp.float32)
    part_sum = lax.dot_general(
        ones, pairs[...], (((1,), (1,)), ((), ())), precision=lax.Precision.HIGHEST,
        preferred_element_type=jnp.float32,
    )

    def total_of(value, slots, send, recv, axis, me, count):
        slots[me] = value
        copies = []
        for d in range(1, count):
            target = lax.rem(me + d, count)
            gz, gy = (target, h) if axis == "gz" else (g, target)
            copy = remote(slots.at[me], slots.at[me], send.at[d - 1], recv.at[d - 1], gz, gy)
            copy.start()
            copies.append(copy)
        for d in range(1, count):
            source = lax.rem(me - d + count, count)
            gz, gy = (source, h) if axis == "gz" else (g, source)
            remote(slots.at[source], slots.at[source], send.at[d - 1], recv.at[d - 1], gz, gy).wait_recv()
        result = slots[0]
        for d in range(1, count):
            result = result + slots[d]
        for copy in copies:
            copy.wait_send()
        return result

    if direct:
        parts[me] = part_sum[0:1]

        def share(d, gz, gy, row):
            return remote(parts.at[row], parts.at[row], pas.at[d - 1], par.at[d - 1], gz, gy)

        for d in range(1, count):
            share(d, *peer(d), me).start()
        for d in range(1, count):
            gz, gy = peer(count - d)
            share(d, gz, gy, gz * ny + gy).wait_recv()
        rows_in = [parts[d] for d in range(count)]
        while len(rows_in) > 1:
            rows_in = [sum(rows_in[d : d + 2]) for d in range(0, len(rows_in), 2)]
        gram_out[...] = jnp.broadcast_to(rows_in[0], gram_out.shape)
        for d in range(1, count):
            share(d, *peer(d), me).wait_send()
    else:
        slab = total_of(part_sum, gsum_y, gys, gyr, "gy", h, ny)
        gram_out[...] = total_of(slab, gsum_z, gzs, gzr, "gz", g, nz)

    sent(mine)
    for i in order:
        for k in range(CHUNKS):
            swap(i, k).wait_send()
    for v in range(mine):
        give_back(v).wait_send()


def filter_and_gram(block, conduct):
    nz, ny = lax.axis_size("gz"), lax.axis_size("gy")
    vectors, planes, rows, columns = block.shape
    mine, span, tall = vectors // 2, 4 * planes, rows + 2 * TILE
    f32 = jnp.float32
    dma = pltpu.SemaphoreType.DMA
    volume = pltpu.VMEM((span, tall, columns), f32)
    return pl.pallas_call(
        functools.partial(kernel, nz, ny),
        out_shape=[jax.ShapeDtypeStruct(block.shape, f32), jax.ShapeDtypeStruct((8, 128), f32)],
        in_specs=[pl.BlockSpec(memory_space=pltpu.HBM)] * 2,
        out_specs=[pl.BlockSpec(memory_space=pltpu.VMEM)] * 2,
        scratch_shapes=[
            pltpu.VMEM((mine, span, tall, columns), f32),
            volume, volume, volume, volume, volume, volume, volume,
            pltpu.VMEM((128, 128), f32),
            pltpu.VMEM((ny, 8, 128), f32),
            pltpu.VMEM((nz, 8, 128), f32),
            pltpu.VMEM((min(nz * ny, DIRECT), 1, 128), f32),
            pltpu.VMEM((mine + 1, planes, rows, columns), f32),
            dma((mine + 1,)), dma((mine + 1,)),
            dma((mine + 1, CHUNKS)), dma((mine + 1, CHUNKS)),
            dma((mine + 1,)), dma((mine + 1,)),
            dma((mine + 1, CHUNKS)), dma((mine + 1, CHUNKS)),
            dma((mine + 1, 4, 2)), dma((mine + 1, 4, 2)),
            dma((mine,)), dma((mine,)), dma((mine,)),
            dma((ny,)), dma((ny,)), dma((nz,)), dma((nz,)),
            dma((min(nz * ny, DIRECT),)), dma((min(nz * ny, DIRECT),)),
        ],
        compiler_params=pltpu.CompilerParams(
            collective_id=0, has_side_effects=True, vmem_limit_bytes=51 * 1024 * 1024
        ),
        name="filter_and_gram",
    )(block, conduct)


def finish_kernel(cells, sums, held, basis, result, given):
    vectors, planes, rows, columns = held.shape
    give = [pltpu.make_async_copy(result.at[:, z], basis.at[:, z], given.at[z]) for z in range(planes)]
    gram = sums[...]
    low = {}
    factors = {}
    recip = []
    for j in range(vectors):
        for i in range(j, vectors):
            at = i * vectors + j
            value = jnp.broadcast_to(gram[:, at : at + 1], (8, 128))
            for k in range(j):
                value = value - low[i, k] * low[j, k]
            if i == j:
                low[j, j] = jnp.sqrt(value)
                recip.append(1.0 / low[j, j])
            else:
                low[i, j] = value * recip[j]
    for j in range(vectors):
        column = {j: recip[j]}
        for i in range(j + 1, vectors):
            value = low[i, j] * column[j]
            for k in range(j + 1, i):
                value = value + low[i, k] * column[k]
            column[i] = -value * recip[i]
        for i in range(j, vectors):
            factors[i, j] = column[i] * math.sqrt(cells)

    for z in range(planes):
        @pl.loop(0, rows, step=8)
        def _(r):
            r = pl.multiple_of(r, 8)
            for c in range(0, columns, 128):
                vals = [held[v, z, pl.ds(r, 8), c : c + 128] for v in range(vectors)]
                for i in range(vectors):
                    total = factors[i, 0] * vals[0]
                    for j in range(1, i + 1):
                        total = total + factors[i, j] * vals[j]
                    result[i, z, pl.ds(r, 8), c : c + 128] = total

        give[z].start()
    for z in range(planes):
        give[z].wait()


def shards(block, conduct):
    vectors, planes, rows, columns = block.shape
    field, sums = filter_and_gram(block, conduct)
    total_cells = columns * rows * planes * lax.axis_size("gz") * lax.axis_size("gy")
    return pl.pallas_call(
        functools.partial(finish_kernel, total_cells),
        out_shape=jax.ShapeDtypeStruct(block.shape, jnp.float32),
        in_specs=[pl.BlockSpec(memory_space=pltpu.VMEM)] * 2,
        out_specs=pl.BlockSpec(memory_space=pltpu.HBM),
        scratch_shapes=[pltpu.VMEM(block.shape, jnp.float32), pltpu.SemaphoreType.DMA((planes,))],
        compiler_params=pltpu.CompilerParams(vmem_limit_bytes=40 * 1024 * 1024),
        name="finish",
    )(sums, field)


def solution(mesh):
    in_specs = (P(None, "gz", "gy", None), P("gz", "gy", None))
    out_specs = P(None, "gz", "gy", None)
    return jax.shard_map(shards, mesh=mesh, in_specs=in_specs, out_specs=out_specs, check_vma=False)
```
